32 devices in a mesh: rep: 1, ep: 32 (over z, y, x, core), hid: 1.
Axes of the slice: x: 2, y: 2, z: 4, core: 2. Of those that a mesh axis runs over, the one named last changes fastest.
Arguments:
- tokens: bfloat16 [4096, 2048], P(('rep', 'ep')), may hold values from -6 to 6
- cotangent: bfloat16 [4096, 2048], P(('rep', 'ep')), may hold values from -2 to 2
- routing: float32 [4096, 8], P(('rep', 'ep')), may hold values from 0.05 to 0.5
- expert_ids: int32 [4096, 8], P(('rep', 'ep')), may hold values from 0 to 63, all different within a row; in each aligned block of 128 rows (0 to 127, 128 to 255, ...) at most 20 rows name the same one
- gate_weight: bfloat16 [64, 2048, 768], P('ep', None, 'hid'), may hold values from -0.125 to 0.125
- up_weight: bfloat16 [64, 2048, 768], P('ep', None, 'hid'), may hold values from -0.125 to 0.125
- down_weight: bfloat16 [64, 768, 2048], P('ep', 'hid'), may hold values from -0.21875 to 0.21875
Outputs:
- input_grad: float32 [4096, 2048], P(('rep', 'ep'), 'hid')
- gate_grad: float32 [4096, 8], P(('rep', 'ep'))
The draws below stay inside these ranges and needn't reach their ends.
Inputs may be any that keep to these rules, and one draw needn't show every extreme that they name: `expert_ids`: among the 128 tokens of one index of ep (aligned blocks of rows), no expert is picked more than 20 times, a bound that some block reaches; the 8 picks of a token are different experts.
All inputs are finite; a program needn't handle non-finite values.
Results may differ from the reference program's by a relative error of at most 0.0029.
Values may be sent and summed in bfloat16 or wider, within the bound.
A program may use at most 128 MiB of HBM per device.

```python
import math
import jax
import jax.numpy as jnp
import numpy as np
from jax import lax

D = 2048
FF = 768
TOP = 8
TOK_DEV = 128
EXPERTS = 64
TOKENS = 4096
CAP = 20
N_EP = 32


def levels(rng, shape, split, smallest, high):
    factor_of, own = 1.0, jax.random.fold_in(rng, 6)
    for position, parts in split:
        heights = jnp.exp(jax.random.uniform(jax.random.fold_in(own, position), (parts,), jnp.float32, smallest / len(split), high / len(split)))
        factor_of = factor_of * jnp.repeat(heights, shape[position] // parts).reshape([-1 if axis == position else 1 for axis in range(len(shape))])
    return factor_of


def deal_out(own_key, own, number, rows, count, top, bound, skew):
    ranking = jax.random.permutation(own_key, count)
    crowded, common = load_shares(count, rows * top, bound, skew, True), load_shares(count, rows * top, bound, skew, False)
    places = jnp.arange(count)

    def named(sizes, offset_by):
        used = int((sizes > 0).sum())
        fixed = max(1, used // 4)
        moved = fixed + (places - fixed + offset_by * (used - fixed)) % max(1, count - fixed)
        return jnp.zeros((count,), jnp.int32).at[ranking[jnp.where(places < fixed, places, moved)]].set(jnp.asarray(sizes, jnp.int32))

    sizes = jnp.where(number % 4 == 0, named(crowded, number // 4), named(common, number - number // 4 - 1))
    mixed = jax.random.permutation(jax.random.fold_in(own, 3), count)
    source_of, receiver = mixed[0:count // 2 * 2:2], mixed[1:count // 2 * 2:2]
    slack = jnp.minimum(sizes[source_of] - 1, bound - sizes[receiver]) // 2
    slack = jnp.where((source_of == ranking[0]) | (receiver == ranking[0]) | (sizes[receiver] == 0), 0, jnp.maximum(slack, 0))
    moved = jax.random.randint(jax.random.fold_in(own, 4), (count // 2,), 0, 1 << 20) % (slack + 1)
    sizes = sizes.at[source_of].add(-moved).at[receiver].add(moved)
    items = jnp.searchsorted(jnp.cumsum(sizes), jnp.arange(rows * top), side="right").astype(jnp.int32)
    table = items.reshape(top, rows).T
    table = table[jax.random.permutation(jax.random.fold_in(own, 1), rows)]
    offset_by = jax.random.randint(jax.random.fold_in(own, 2), (rows, 1), 0, top)
    return jnp.take_along_axis(table, (jnp.arange(top)[None, :] + offset_by) % top, axis=1)


def load_shares(number_of, total, most, lean, full):
    weights = [(1 << 20) // math.isqrt(rank ** lean) + 1 for rank in range(1, number_of + 1)]
    largest = most if full else min(most, max(-(-total // number_of), total * weights[0] // sum(weights)))
    least = 1 if total - largest >= number_of - 1 else 0
    holding, spare = [largest] + [least] * (number_of - 1), total - largest - least * (number_of - 1)
    while spare > 0:
        candidates = [i for i in range(1, number_of) if holding[i] < largest] or [i for i in range(1, number_of) if holding[i] < most]
        whole, left = sum([weights[i] for i in candidates]), spare
        for i in candidates:
            more = min(most - holding[i], max(1, left * weights[i] // whole), spare)
            holding[i] = holding[i] + more
            spare = spare - more
    return np.array(holding)


def bell_draw(rng, dims, deviation, bound, pieces=(), kind=jnp.bfloat16):
    gain = levels(rng, dims, pieces, -0.22, 0.18) if pieces else 1.0
    entries = jax.random.normal(rng, dims, jnp.float32) * deviation * gain
    return jnp.minimum(jnp.maximum(entries, -bound), bound).astype(kind)


def setup_inputs(seed: int = 0, part: int = 0) -> dict:
    arg_keys = jax.random.split(jax.random.key(seed), 8)
    own_keys = jax.random.split(jax.random.fold_in(arg_keys[7], part), 8)
    tokens = bell_draw(own_keys[0], (TOKENS, D), 1.0, 6.0, ((0, 32),))
    cotangent = bell_draw(own_keys[1], (TOKENS, D), 0.3, 2.0, ((0, 32),))
    routing = jnp.clip(jnp.exp(math.log(0.5) - 2.3025851 * jax.random.uniform(own_keys[2], (TOKENS, TOP), jnp.float32) ** levels(own_keys[2], (TOKENS, TOP), ((0, 32),), -0.2, 0.2)), 0.05, 0.5)
    expert_ids_keys = jax.random.split(jax.random.fold_in(own_keys[3], 1), TOKENS // TOK_DEV)
    expert_ids_turns = jax.random.permutation(jax.random.fold_in(own_keys[3], 3), TOKENS // TOK_DEV)
    expert_ids = jax.vmap(lambda own, number: deal_out(jax.random.fold_in(own_keys[3], 2), own, number, TOK_DEV, EXPERTS, TOP, CAP, 1))(expert_ids_keys, expert_ids_turns).reshape((TOKENS, TOP))
    gate_weight = bell_draw(arg_keys[4], (EXPERTS, D, FF), D ** -0.5, 0.125, ((0, 32),))
    up_weight = bell_draw(arg_keys[5], (EXPERTS, D, FF), D ** -0.5, 0.125, ((0, 32),))
    down_weight = bell_draw(arg_keys[6], (EXPERTS, FF, D), FF ** -0.5, 0.21875, ((0, 32),))
    return dict(tokens=tokens, cotangent=cotangent, routing=routing, expert_ids=expert_ids, gate_weight=gate_weight, up_weight=up_weight, down_weight=down_weight)


def slot_rank(flat, experts):
    onehot = (flat[:, None] == jnp.arange(experts, dtype=jnp.int32)[None, :]).astype(jnp.int32)
    before = jnp.cumsum(onehot, axis=0) - onehot
    return jnp.sum(before * onehot, axis=1).astype(jnp.int32)


def reference(tokens, cotangent, routing, expert_ids, gate_weight, up_weight, down_weight):
    picks = TOK_DEV * TOP
    rows_expert = N_EP * CAP
    id_blocks = expert_ids.reshape(N_EP, picks).astype(jnp.int32)
    ranks = jax.vmap(lambda flat: slot_rank(flat, EXPERTS))(id_blocks)
    source = jnp.arange(N_EP, dtype=jnp.int32)[:, None]
    slots = (id_blocks * rows_expert + source * CAP + ranks).reshape(-1).astype(jnp.int32)
    pick_index = jnp.arange(TOKENS * TOP, dtype=jnp.int32)
    token_index = (pick_index // TOP).astype(jnp.int32)
    slot_token = jnp.full((EXPERTS * rows_expert,), TOKENS, jnp.int32).at[slots].set(token_index)
    slot_pick = jnp.full((EXPERTS * rows_expert,), TOKENS * TOP, jnp.int32).at[slots].set(pick_index)
    padding = jnp.zeros((1, D), tokens.dtype)
    token_rows = jnp.concatenate([tokens, padding], 0)[slot_token].reshape(EXPERTS, rows_expert, D)
    cotan_rows = jnp.concatenate([cotangent, padding], 0)[slot_token].reshape(EXPERTS, rows_expert, D)
    weight_flat = jnp.concatenate([routing.reshape(-1), jnp.zeros((1,), jnp.float32)], 0)
    slot_weight = weight_flat[slot_pick].reshape(EXPERTS, rows_expert)
    slot_token = slot_token.reshape(EXPERTS, rows_expert)
    slot_pick = slot_pick.reshape(EXPERTS, rows_expert)

    def expert_step(carry, items):
        grad_sum, gate_sum = carry
        inputs, grads_in, w_gate, up_proj, w_down, target, pick_slot, weight = items
        gate_pre = jnp.dot(inputs, w_gate, preferred_element_type=jnp.float32)
        up_pre = jnp.dot(inputs, up_proj, preferred_element_type=jnp.float32)
        upward = jnp.dot(grads_in, w_down.T, preferred_element_type=jnp.float32)
        sigma = jax.nn.sigmoid(gate_pre)
        silu_val = gate_pre * sigma
        hidden = silu_val * up_pre
        pick_gate = jnp.sum(hidden * upward, axis=1)
        gate_delta = (upward * up_pre * sigma * (1.0 + gate_pre * (1.0 - sigma))).astype(jnp.bfloat16)
        up_delta = (upward * silu_val).astype(jnp.bfloat16)
        pick_grad = jnp.dot(gate_delta, w_gate.T, preferred_element_type=jnp.float32)
        pick_grad = pick_grad + jnp.dot(up_delta, up_proj.T, preferred_element_type=jnp.float32)
        grad_sum = grad_sum.at[target].add(weight[:, None] * pick_grad, mode="drop")
        gate_sum = gate_sum.at[pick_slot].add(pick_gate, mode="drop")
        return (grad_sum, gate_sum), None

    start = (jnp.zeros((TOKENS, D), jnp.float32), jnp.zeros((TOKENS * TOP,), jnp.float32))
    (grad_sum, gate_sum), _ = lax.scan(expert_step, start, (token_rows, cotan_rows, gate_weight, up_weight, down_weight, slot_token, slot_pick, slot_weight))
    return grad_sum, gate_sum.reshape(TOKENS, TOP)
```

```python
import jax
import jax.numpy as jnp
from jax import lax
from jax.sharding import PartitionSpec as P

BF = jnp.bfloat16
F32 = jnp.float32


def dot(a, b):
    return jnp.dot(a, b, preferred_element_type=F32)


def split_two(value):
    high = lax.reduce_precision(value, 8, 7)
    return high.astype(BF), (value - high).astype(BF)


def local(tokens, cotangent, routing, expert_ids, gate_weight, up_weight, down_weight):
    count = lax.axis_size("ep")
    owned = gate_weight.shape[0]
    experts = owned * count
    tok_rows, top = expert_ids.shape
    width = tokens.shape[1]
    cap = 5 * tok_rows * top // (4 * experts)
    slots = experts * cap

    onehot = expert_ids[:, :, None] == jnp.arange(experts, dtype=jnp.int32)[None, None, :]
    picked = jnp.any(onehot, axis=1)
    row = jnp.arange(tok_rows, dtype=jnp.int32)
    lower = (row[:, None] > row[None, :]).astype(BF)
    before = dot(lower, picked.astype(BF))
    rank = jnp.where(picked, before, -1.0).astype(BF)
    slot = jnp.arange(slots, dtype=jnp.int32)
    spread = (slot[:, None] // cap == jnp.arange(experts, dtype=jnp.int32)[None, :]).astype(BF)
    place = (slot % cap).astype(F32)
    rank_of = lax.dot_general(spread, rank, (((1,), (1,)), ((), ())), preferred_element_type=F32)
    choose = (rank_of == place[:, None]).astype(BF)
    rank_back = lax.dot_general(rank, spread, (((1,), (1,)), ((), ())), preferred_element_type=F32)
    choose_back = rank_back == place[None, :]

    def exchange(value):
        return lax.all_to_all(value, "ep", split_axis=0, concat_axis=0, tiled=True)

    def by_expert(value):
        value = value.reshape(count, owned, cap, value.shape[1])
        return value.transpose(1, 0, 2, 3).reshape(owned, count * cap, value.shape[3])

    def by_source(value):
        value = value.reshape(owned, count, cap, value.shape[2])
        return value.transpose(1, 0, 2, 3).reshape(slots, value.shape[3])

    inputs = by_expert(exchange(dot(choose, tokens).astype(BF)))
    grads_in = by_expert(exchange(dot(choose, cotangent).astype(BF)))
    gate_pre = jnp.einsum("erd,edf->erf", inputs, gate_weight, preferred_element_type=F32)
    up_pre = jnp.einsum("erd,edf->erf", inputs, up_weight, preferred_element_type=F32)
    upward = jnp.einsum("erd,efd->erf", grads_in, down_weight, preferred_element_type=F32)
    sigma = jax.nn.sigmoid(gate_pre)
    silu_val = gate_pre * sigma
    pick_gate = jnp.sum(silu_val * up_pre * upward, axis=2, keepdims=True)
    gate_delta = (upward * up_pre * sigma * (1.0 + gate_pre * (1.0 - sigma))).astype(BF)
    up_delta = (upward * silu_val).astype(BF)
    deltas = jnp.concatenate([gate_delta, up_delta], axis=2)
    joined = jnp.concatenate([gate_weight, up_weight], axis=2)

    half = width // 2
    gate_high, gate_low = split_two(pick_gate)
    lane = jnp.arange(128, dtype=jnp.int32)[None, None, :]
    gate_cols = jnp.where(lane == 0, gate_high, jnp.where(lane == 1, gate_low, jnp.zeros((), BF)))
    first = jnp.einsum("erf,edf->erd", deltas, joined[:, :half], preferred_element_type=F32).astype(BF)
    second = jnp.einsum("erf,edf->erd", deltas, joined[:, half:], preferred_element_type=F32).astype(BF)
    back_a = exchange(by_source(jnp.concatenate([first, gate_cols], axis=2)))
    back_b = exchange(by_source(second))

    amount = jnp.sum(jnp.where(onehot, routing[:, :, None], 0.0), axis=1)
    amount_high, amount_low = split_two(amount)
    zero = jnp.zeros((), BF)

    def mix(part):
        wide = lax.dot_general(part, spread, (((1,), (1,)), ((), ())), preferred_element_type=F32)
        return jnp.where(choose_back, wide.astype(BF), zero)

    mixing = jnp.concatenate([mix(amount_high), mix(amount_low)], axis=0)

    def combine(value):
        both = dot(mixing, value)
        return both[:tok_rows] + both[tok_rows:]

    weighted = jnp.concatenate([combine(back_a[:, :half]), combine(back_b)], axis=1)
    gates = back_a[:, half:half + 2].T

    def gate_part(i):
        return dot(jnp.where(choose_back, gates[i][None, :], zero), spread)

    gate_sum = gate_part(0) + gate_part(1)
    gate_grad = jnp.sum(jnp.where(onehot, gate_sum[:, None, :], 0.0), axis=2)
    input_grad = lax.psum_scatter(weighted, "hid", scatter_dimension=1, tiled=True)
    return (input_grad, lax.psum(gate_grad, "hid"))


def solution(mesh):
    placed = (
        P(("rep", "ep"), None),
        P(("rep", "ep"), None),
        P(("rep", "ep"), None),
        P(("rep", "ep"), None),
        P("ep", None, "hid"),
        P("ep", None, "hid"),
        P("ep", "hid", None),
    )
    return jax.shard_map(
        local,
        mesh=mesh,
        in_specs=placed,
        out_specs=(P(("rep", "ep"), "hid"), P(("rep", "ep"), None)),
        check_vma=False,
    )
```

```python
import functools

import jax
import jax.numpy as jnp
from jax import lax
from jax.experimental import pallas as pl
from jax.experimental.pallas import tpu as pltpu
from jax.sharding import PartitionSpec as P

BF = jnp.bfloat16
F32 = jnp.float32


def dot(a, b):
    return jnp.dot(a, b, preferred_element_type=F32)


def split_two(value):
    high = lax.reduce_precision(value, 8, 7)
    return high.astype(BF), (value - high).astype(BF)


def flipped(value, bits):
    result, weight = value * 0, 1
    while weight <= bits:
        digit = lax.rem(lax.div(value, weight), 2)
        result = result + weight * ((1 - digit) if bits & weight else digit)
        weight *= 2
    return result + weight * lax.div(value, weight)


def gather_kernel(planes, block_ref, all_ref, own_sem, far_sem, send_sem, recv_sem):
    me = lax.axis_index("ep")
    z, rest = lax.div(me, 8), lax.rem(me, 8)

    def at(k, bits):
        return flipped(z, k) * 8 + flipped(rest, bits)

    barrier = pltpu.get_barrier_semaphore()
    partners = [at(k, 0) for k in range(1, planes)] + [at(0, b) for b in (1, 2, 4)]
    for other in partners:
        pl.semaphore_signal(
            barrier, inc=1, device_id={"ep": other}, device_id_type=pl.DeviceIdType.MESH
        )
    pl.semaphore_wait(barrier, len(partners))

    own = pltpu.make_async_copy(block_ref, all_ref.at[me], own_sem)
    own.start()
    started = []

    def send(source, slot, sem, other):
        copy = pltpu.make_async_remote_copy(
            src_ref=source,
            dst_ref=all_ref.at[slot],
            send_sem=sem,
            recv_sem=recv_sem.at[slot],
            device_id={"ep": other},
            device_id_type=pl.DeviceIdType.MESH,
        )
        copy.start()
        started.append(copy)

    def arrived(slot):
        pltpu.make_async_remote_copy(
            src_ref=block_ref,
            dst_ref=all_ref.at[slot],
            send_sem=own_sem,
            recv_sem=recv_sem.at[slot],
            device_id={"ep": at(0, 1)},
            device_id_type=pl.DeviceIdType.MESH,
        ).wait_recv()

    def forward(slot, bits):
        for i, b in enumerate((2, 4, 1)):
            if b in bits:
                send(all_ref.at[slot], slot, send_sem.at[slot, i], at(0, b))

    send(block_ref, me, far_sem.at[0], at(1, 0))
    for i, b in enumerate((2, 4, 1)):
        send(block_ref, me, send_sem.at[me, i], at(0, b))
    for k in range(2, planes):
        send(block_ref, me, far_sem.at[k - 1], at(k, 0))

    def plane(k):
        along_x, along_y = at(k, 2), at(k, 4)
        even = k % 2 == 0
        arrived(along_x)
        forward(along_x, (1,) if even else (4, 1))
        arrived(along_y)
        forward(along_y, (2, 1) if even else (1,))

    for k in range(1, planes):
        arrived(at(k, 0))
        forward(at(k, 0), (2, 4, 1))
        plane(k - 1)
    plane(planes - 1)
    for k in range(planes):
        arrived(at(k, 6))
        forward(at(k, 6), (1,))
    for k in range(planes):
        for b in (1, 3, 5, 7):
            arrived(at(k, b))
    own.wait()
    for copy in started:
        copy.wait_send()


def gather_blocks(block, count):
    planes = count // 8
    return pl.pallas_call(
        functools.partial(gather_kernel, planes),
        out_shape=jax.ShapeDtypeStruct((count,) + block.shape, block.dtype),
        in_specs=[pl.BlockSpec(memory_space=pltpu.VMEM)],
        out_specs=pl.BlockSpec(memory_space=pl.ANY),
        scratch_shapes=[
            pltpu.SemaphoreType.DMA,
            pltpu.SemaphoreType.DMA((planes - 1,)),
            pltpu.SemaphoreType.DMA((count, 3)),
            pltpu.SemaphoreType.DMA((count,)),
        ],
        compiler_params=pltpu.CompilerParams(collective_id=0, has_side_effects=True),
    )(block)


def owner_rows(tokens, cotangent, picked, lower, owned, cap, count):
    tok_rows, width = tokens.shape
    experts = picked.shape[1]
    lanes = -(-experts // 128) * 128
    marks = jnp.pad(picked.astype(BF), ((0, 0), (0, lanes - experts)))
    every = gather_blocks(jnp.concatenate([tokens, cotangent, marks], axis=1), count)
    marks = every[:, :, 2 * width:]
    before = jnp.einsum("ut,ste->sue", lower, marks, preferred_element_type=F32)
    rank = jnp.where(marks > 0, before, -1.0).astype(BF).reshape(count * tok_rows, lanes)
    mine = lax.axis_index("ep") * owned + jnp.arange(owned, dtype=jnp.int32)
    chosen = (mine[:, None] == jnp.arange(lanes, dtype=jnp.int32)[None, :]).astype(BF)
    rank_of = lax.dot_general(chosen, rank, (((1,), (1,)), ((), ())), preferred_element_type=F32)
    group = 4
    rank_of = rank_of.reshape(owned, count // group, 1, group * tok_rows)
    slot = jnp.arange(group * cap, dtype=jnp.int32)[:, None]
    token = jnp.arange(group * tok_rows, dtype=jnp.int32)[None, :]
    same = slot // cap == token // tok_rows
    choose = (same & (rank_of == (slot % cap).astype(F32))).astype(BF)
    every = every.reshape(count // group, group * tok_rows, every.shape[2])

    def take(columns):
        rows = [
            jnp.einsum("gru,gud->grd", choose[j], columns, preferred_element_type=F32)
            .astype(BF).reshape(count * cap, width)
            for j in range(owned)
        ]
        return rows

    return take(every[:, :, :width]), take(every[:, :, width:2 * width])


def local(direct, tokens, cotangent, routing, expert_ids, gate_weight, up_weight, down_weight):
    count = lax.axis_size("ep")
    owned = gate_weight.shape[0]
    experts = owned * count
    tok_rows, top = expert_ids.shape
    width = tokens.shape[1]
    cap = 5 * tok_rows * top // (4 * experts)
    slots = experts * cap

    onehot = expert_ids[:, :, None] == jnp.arange(experts, dtype=jnp.int32)[None, None, :]
    picked = jnp.any(onehot, axis=1)
    row = jnp.arange(tok_rows, dtype=jnp.int32)
    lower = (row[:, None] > row[None, :]).astype(BF)
    before = dot(lower, picked.astype(BF))
    rank = jnp.where(picked, before, -1.0).astype(BF)
    slot = jnp.arange(slots, dtype=jnp.int32)
    spread = (slot[:, None] // cap == jnp.arange(experts, dtype=jnp.int32)[None, :]).astype(BF)
    place = (slot % cap).astype(F32)
    rank_of = lax.dot_general(spread, rank, (((1,), (1,)), ((), ())), preferred_element_type=F32)
    choose = (rank_of == place[:, None]).astype(BF)
    rank_back = lax.dot_general(rank, spread, (((1,), (1,)), ((), ())), preferred_element_type=F32)
    choose_back = rank_back == place[None, :]

    def exchange(value):
        return lax.all_to_all(value, "ep", split_axis=0, concat_axis=0, tiled=True)

    def by_expert(value):
        value = value.reshape(count, owned, cap, value.shape[1])
        return value.transpose(1, 0, 2, 3).reshape(owned, count * cap, value.shape[3])

    def by_source(value):
        value = value.reshape(owned, count, cap, value.shape[2])
        return value.transpose(1, 0, 2, 3).reshape(slots, value.shape[3])

    if direct:
        inputs, grads_in = owner_rows(tokens, cotangent, picked, lower, owned, cap, count)
        inputs, grads_in = jnp.stack(inputs), jnp.stack(grads_in)
    else:
        inputs = by_expert(exchange(dot(choose, tokens).astype(BF)))
        grads_in = by_expert(exchange(dot(choose, cotangent).astype(BF)))
    gate_pre = jnp.einsum("erd,edf->erf", inputs, gate_weight, preferred_element_type=F32)
    up_pre = jnp.einsum("erd,edf->erf", inputs, up_weight, preferred_element_type=F32)
    upward = jnp.einsum("erd,efd->erf", grads_in, down_weight, preferred_element_type=F32)
    sigma = jax.nn.sigmoid(gate_pre)
    silu_val = gate_pre * sigma
    pick_gate = jnp.sum(silu_val * up_pre * upward, axis=2, keepdims=True)
    gate_delta = (upward * up_pre * sigma * (1.0 + gate_pre * (1.0 - sigma))).astype(BF)
    up_delta = (upward * silu_val).astype(BF)
    deltas = jnp.concatenate([gate_delta, up_delta], axis=2)
    joined = jnp.concatenate([gate_weight, up_weight], axis=2)

    half = width // 2
    gate_high, gate_low = split_two(pick_gate)
    lane = jnp.arange(128, dtype=jnp.int32)[None, None, :]
    gate_cols = jnp.where(lane == 0, gate_high, jnp.where(lane == 1, gate_low, jnp.zeros((), BF)))
    first = jnp.einsum("erf,edf->erd", deltas, joined[:, :half], preferred_element_type=F32).astype(BF)
    second = jnp.einsum("erf,edf->erd", deltas, joined[:, half:], preferred_element_type=F32).astype(BF)
    back_a = exchange(by_source(jnp.concatenate([first, gate_cols], axis=2)))
    back_b = exchange(by_source(second))

    amount = jnp.sum(jnp.where(onehot, routing[:, :, None], 0.0), axis=1)
    amount_high, amount_low = split_two(amount)
    zero = jnp.zeros((), BF)

    def mix(part):
        wide = lax.dot_general(part, spread, (((1,), (1,)), ((), ())), preferred_element_type=F32)
        return jnp.where(choose_back, wide.astype(BF), zero)

    mixing = jnp.concatenate([mix(amount_high), mix(amount_low)], axis=0)

    def combine(value):
        both = dot(mixing, value)
        return both[:tok_rows] + both[tok_rows:]

    weighted = jnp.concatenate([combine(back_a[:, :half]), combine(back_b)], axis=1)
    gates = back_a[:, half:half + 2].T

    def gate_part(i):
        return dot(jnp.where(choose_back, gates[i][None, :], zero), spread)

    gate_sum = gate_part(0) + gate_part(1)
    gate_grad = jnp.sum(jnp.where(onehot, gate_sum[:, None, :], 0.0), axis=2)
    input_grad = lax.psum_scatter(weighted, "hid", scatter_dimension=1, tiled=True)
    return (input_grad, lax.psum(gate_grad, "hid"))


def solution(mesh):
    placed = (
        P(("rep", "ep"), None),
        P(("rep", "ep"), None),
        P(("rep", "ep"), None),
        P(("rep", "ep"), None),
        P("ep", None, "hid"),
        P("ep", None, "hid"),
        P("ep", "hid", None),
    )
    count = mesh.shape["ep"]
    planes = count // 8
    direct = (
        mesh.shape["rep"] * mesh.shape["hid"] == 1
        and count % 8 == 0
        and planes > 1
        and planes & (planes - 1) == 0
    )
    return jax.shard_map(
        functools.partial(local, direct),
        mesh=mesh,
        in_specs=placed,
        out_specs=(P(("rep", "ep"), "hid"), P(("rep", "ep"), None)),
        check_vma=False,
    )
```

```python
import functools

import jax
import jax.numpy as jnp
from jax import lax
from jax.experimental import pallas as pl
from jax.experimental.pallas import tpu as pltpu
from jax.sharding import PartitionSpec as P

BF = jnp.bfloat16
F32 = jnp.float32


def dot(a, b):
    return jnp.dot(a, b, preferred_element_type=F32)


def split_two(value):
    high = lax.reduce_precision(value, 8, 7)
    return high.astype(BF), (value - high).astype(BF)


def flipped(value, bits):
    result, weight = value * 0, 1
    while weight <= bits:
        digit = lax.rem(lax.div(value, weight), 2)
        result = result + weight * ((1 - digit) if bits & weight else digit)
        weight *= 2
    return result + weight * lax.div(value, weight)


def gather_kernel(planes, block_ref, all_ref, own_sem, far_sem, send_sem, recv_sem):
    me = lax.axis_index("ep")
    z, rest = lax.div(me, 8), lax.rem(me, 8)

    def at(k, bits):
        return flipped(z, k) * 8 + flipped(rest, bits)

    barrier = pltpu.get_barrier_semaphore()
    partners = [at(k, 0) for k in range(1, planes)] + [at(0, b) for b in (1, 2, 4)]
    for other in partners:
        pl.semaphore_signal(
            barrier, inc=1, device_id={"ep": other}, device_id_type=pl.DeviceIdType.MESH
        )
    pl.semaphore_wait(barrier, len(partners))

    own = pltpu.make_async_copy(block_ref, all_ref.at[me], own_sem)
    own.start()
    started = []

    def send(source, slot, sem, other):
        copy = pltpu.make_async_remote_copy(
            src_ref=source,
            dst_ref=all_ref.at[slot],
            send_sem=sem,
            recv_sem=recv_sem.at[slot],
            device_id={"ep": other},
            device_id_type=pl.DeviceIdType.MESH,
        )
        copy.start()
        started.append(copy)

    def arrived(slot):
        pltpu.make_async_remote_copy(
            src_ref=block_ref,
            dst_ref=all_ref.at[slot],
            send_sem=own_sem,
            recv_sem=recv_sem.at[slot],
            device_id={"ep": at(0, 1)},
            device_id_type=pl.DeviceIdType.MESH,
        ).wait_recv()

    def forward(slot, bits):
        for i, b in enumerate((2, 4, 1)):
            if b in bits:
                send(all_ref.at[slot], slot, send_sem.at[slot, i], at(0, b))

    send(block_ref, me, far_sem.at[0], at(1, 0))
    for i, b in enumerate((2, 4, 1)):
        send(block_ref, me, send_sem.at[me, i], at(0, b))
    for k in range(2, planes):
        send(block_ref, me, far_sem.at[k - 1], at(k, 0))

    def plane(k):
        along_x, along_y = at(k, 2), at(k, 4)
        even = k % 2 == 0
        arrived(along_x)
        forward(along_x, (1,) if even else (4, 1))
        arrived(along_y)
        forward(along_y, (2, 1) if even else (1,))

    for k in range(1, planes):
        arrived(at(k, 0))
        forward(at(k, 0), (2, 4, 1))
        plane(k - 1)
    plane(planes - 1)
    for k in range(planes):
        arrived(at(k, 6))
        forward(at(k, 6), (1,))
    for k in range(planes):
        for b in (1, 3, 5, 7):
            arrived(at(k, b))
    own.wait()
    for copy in started:
        copy.wait_send()


def gather_blocks(block, count):
    planes = count // 8
    return pl.pallas_call(
        functools.partial(gather_kernel, planes),
        out_shape=jax.ShapeDtypeStruct((count,) + block.shape, block.dtype),
        in_specs=[pl.BlockSpec(memory_space=pltpu.VMEM)],
        out_specs=pl.BlockSpec(memory_space=pl.ANY),
        scratch_shapes=[
            pltpu.SemaphoreType.DMA,
            pltpu.SemaphoreType.DMA((planes - 1,)),
            pltpu.SemaphoreType.DMA((count, 3)),
            pltpu.SemaphoreType.DMA((count,)),
        ],
        compiler_params=pltpu.CompilerParams(collective_id=0, has_side_effects=True),
    )(block)


def owner_rows(tokens, cotangent, picked, lower, owned, cap, count):
    tok_rows, width = tokens.shape
    experts = picked.shape[1]
    lanes = -(-experts // 128) * 128
    marks = jnp.pad(picked.astype(BF), ((0, 0), (0, lanes - experts)))
    every = gather_blocks(jnp.concatenate([tokens, cotangent, marks], axis=1), count)
    marks = every[:, :, 2 * width:]
    before = jnp.einsum("ut,ste->sue", lower, marks, preferred_element_type=F32)
    rank = jnp.where(marks > 0, before, -1.0).astype(BF).reshape(count * tok_rows, lanes)
    mine = lax.axis_index("ep") * owned + jnp.arange(owned, dtype=jnp.int32)
    chosen = (mine[:, None] == jnp.arange(lanes, dtype=jnp.int32)[None, :]).astype(BF)
    rank_of = lax.dot_general(chosen, rank, (((1,), (1,)), ((), ())), preferred_element_type=F32)
    group = 4
    rank_of = rank_of.reshape(owned, count // group, 1, group * tok_rows)
    slot = jnp.arange(group * cap, dtype=jnp.int32)[:, None]
    token = jnp.arange(group * tok_rows, dtype=jnp.int32)[None, :]
    same = slot // cap == token // tok_rows
    choose = (same & (rank_of == (slot % cap).astype(F32))).astype(BF)
    every = every.reshape(count // group, group * tok_rows, every.shape[2])

    choose = jnp.concatenate([choose[j] for j in range(owned)], axis=1)
    height = group * cap

    def take(columns):
        both = jnp.einsum("gru,gud->grd", choose, columns, preferred_element_type=F32).astype(BF)
        return [
            both[:, j * height:(j + 1) * height].reshape(count * cap, width) for j in range(owned)
        ]

    return take(every[:, :, :width]), take(every[:, :, width:2 * width])


def local(direct, tokens, cotangent, routing, expert_ids, gate_weight, up_weight, down_weight):
    count = lax.axis_size("ep")
    owned = gate_weight.shape[0]
    experts = owned * count
    tok_rows, top = expert_ids.shape
    width = tokens.shape[1]
    cap = 5 * tok_rows * top // (4 * experts)
    slots = experts * cap

    onehot = expert_ids[:, :, None] == jnp.arange(experts, dtype=jnp.int32)[None, None, :]
    picked = jnp.any(onehot, axis=1)
    row = jnp.arange(tok_rows, dtype=jnp.int32)
    lower = (row[:, None] > row[None, :]).astype(BF)
    before = dot(lower, picked.astype(BF))
    rank = jnp.where(picked, before, -1.0).astype(BF)
    slot = jnp.arange(slots, dtype=jnp.int32)
    spread = (slot[:, None] // cap == jnp.arange(experts, dtype=jnp.int32)[None, :]).astype(BF)
    place = (slot % cap).astype(F32)
    rank_of = lax.dot_general(spread, rank, (((1,), (1,)), ((), ())), preferred_element_type=F32)
    choose = (rank_of == place[:, None]).astype(BF)
    rank_back = lax.dot_general(rank, spread, (((1,), (1,)), ((), ())), preferred_element_type=F32)
    choose_back = rank_back == place[None, :]

    def exchange(value):
        return lax.all_to_all(value, "ep", split_axis=0, concat_axis=0, tiled=True)

    def by_expert(value):
        value = value.reshape(count, owned, cap, value.shape[1])
        return value.transpose(1, 0, 2, 3).reshape(owned, count * cap, value.shape[3])

    def by_source(value):
        value = value.reshape(owned, count, cap, value.shape[2])
        return value.transpose(1, 0, 2, 3).reshape(slots, value.shape[3])

    if direct:
        inputs, grads_in = owner_rows(tokens, cotangent, picked, lower, owned, cap, count)
        inputs, grads_in = jnp.stack(inputs), jnp.stack(grads_in)
    else:
        inputs = by_expert(exchange(dot(choose, tokens).astype(BF)))
        grads_in = by_expert(exchange(dot(choose, cotangent).astype(BF)))
    gate_pre = jnp.einsum("erd,edf->erf", inputs, gate_weight, preferred_element_type=F32)
    up_pre = jnp.einsum("erd,edf->erf", inputs, up_weight, preferred_element_type=F32)
    upward = jnp.einsum("erd,efd->erf", grads_in, down_weight, preferred_element_type=F32)
    sigma = jax.nn.sigmoid(gate_pre)
    silu_val = gate_pre * sigma
    pick_gate = jnp.sum(silu_val * up_pre * upward, axis=2, keepdims=True)
    gate_delta = (upward * up_pre * sigma * (1.0 + gate_pre * (1.0 - sigma))).astype(BF)
    up_delta = (upward * silu_val).astype(BF)
    deltas = jnp.concatenate([gate_delta, up_delta], axis=2)
    joined = jnp.concatenate([gate_weight, up_weight], axis=2)

    half = width // 2
    gate_high, gate_low = split_two(pick_gate)
    lane = jnp.arange(128, dtype=jnp.int32)[None, None, :]
    gate_cols = jnp.where(lane == 0, gate_high, jnp.where(lane == 1, gate_low, jnp.zeros((), BF)))
    first = jnp.einsum("erf,edf->erd", deltas, joined[:, :half], preferred_element_type=F32).astype(BF)
    second = jnp.einsum("erf,edf->erd", deltas, joined[:, half:], preferred_element_type=F32).astype(BF)
    back_a = exchange(by_source(jnp.concatenate([first, gate_cols], axis=2)))
    back_b = exchange(by_source(second))

    amount = jnp.sum(jnp.where(onehot, routing[:, :, None], 0.0), axis=1)
    amount_high, amount_low = split_two(amount)
    zero = jnp.zeros((), BF)

    def mix(part):
        wide = lax.dot_general(part, spread, (((1,), (1,)), ((), ())), preferred_element_type=F32)
        return jnp.where(choose_back, wide.astype(BF), zero)

    mixing = jnp.concatenate([mix(amount_high), mix(amount_low)], axis=0)

    def combine(value):
        both = dot(mixing, value)
        return both[:tok_rows] + both[tok_rows:]

    weighted = jnp.concatenate([combine(back_a[:, :half]), combine(back_b)], axis=1)
    gates = back_a[:, half:half + 2].T

    def gate_part(i):
        return dot(jnp.where(choose_back, gates[i][None, :], zero), spread)

    gate_sum = gate_part(0) + gate_part(1)
    gate_grad = jnp.sum(jnp.where(onehot, gate_sum[:, None, :], 0.0), axis=2)
    input_grad = lax.psum_scatter(weighted, "hid", scatter_dimension=1, tiled=True)
    return (input_grad, lax.psum(gate_grad, "hid"))


def solution(mesh):
    placed = (
        P(("rep", "ep"), None),
        P(("rep", "ep"), None),
        P(("rep", "ep"), None),
        P(("rep", "ep"), None),
        P("ep", None, "hid"),
        P("ep", None, "hid"),
        P("ep", "hid", None),
    )
    count = mesh.shape["ep"]
    planes = count // 8
    direct = (
        mesh.shape["rep"] * mesh.shape["hid"] == 1
        and count % 8 == 0
        and planes > 1
        and planes & (planes - 1) == 0
    )
    return jax.shard_map(
        functools.partial(local, direct),
        mesh=mesh,
        in_specs=placed,
        out_specs=(P(("rep", "ep"), "hid"), P(("rep", "ep"), None)),
        check_vma=False,
    )
```
